256 devices in a mesh: layer: 4 (over x_lo, core), feat: 64 (over x_hi, z, y).
Axes of the slice: x: 4 (x_hi: 2, x_lo: 2; x = x_hi * 2 + x_lo), y: 4, z: 8, core: 2. Of those that a mesh axis runs over, the one named last changes fastest.
Arguments:
- sources: bfloat16 [4, 512, 4096], P('layer', 'feat'), may hold values from -6 to 6
- targets: bfloat16 [4, 512, 4096], P('layer', 'feat'), may hold values from -6 to 6
- enc_weight: bfloat16 [4, 8192, 4096], P('layer', 'feat'), may hold values from -0.09375 to 0.09375
- dec_weight: bfloat16 [4, 4, 8192, 4096], P('layer', None, 'feat'), may hold values from -0.0625 to 0.0625
- active: int32 [4, 8192, 512], P('layer', 'feat'), may hold values 0 or 1
Outputs:
- errors: float32 [4, 512, 4096], P('layer', 'feat')
- grad_dec: bfloat16 [4, 4, 8192, 4096], P('layer', None, 'feat')
- grad_enc: bfloat16 [4, 8192, 4096], P('layer', 'feat')
The draws below stay inside these ranges and needn't reach their ends.
All inputs are finite; a program needn't handle non-finite values. No bound on the sum of `active` on one device may be relied on, other than what follows from the above.
Results may differ from the reference program's by a relative error of at most 0.0061.
Values may be sent and summed in bfloat16 or wider, within the bound.
No kernel may reach another device: no remote copies, remote signals or barrier semaphores. Data moves between devices by JAX's collectives and lax.ppermute only.
A program may use at most 64 MiB of HBM per device.

```python
import math
import jax
import jax.numpy as jnp

D = 4096
F = 8192
TOKENS = 512
LAYERS = 4


def set_ends(entries, own_key, low, largest):
    place = [jax.random.randint(jax.random.fold_in(own_key, axis), (), 0, length) for axis, length in enumerate(entries.shape)]
    longest = entries.shape.index(max(entries.shape))
    neighbour = place[:longest] + [(place[longest] + 1) % entries.shape[longest]] + place[longest + 1:]
    return entries.at[tuple(place)].set(low).at[tuple(neighbour)].set(largest)


def level_of(stream_key, dims, cuts, smallest, high):
    gain, own = 1.0, jax.random.fold_in(stream_key, 6)
    for dim, blocks in cuts:
        steps = jnp.exp(jax.random.uniform(jax.random.fold_in(own, dim), (blocks,), jnp.float32, smallest / len(cuts), high / len(cuts)))
        gain = gain * jnp.repeat(steps, dims[dim] // blocks).reshape([-1 if axis == dim else 1 for axis in range(len(dims))])
    return gain


def noise(own_key, dims, width, most, pieces=(), dtype=jnp.bfloat16):
    values = jax.random.normal(own_key, dims, jnp.float32) * width
    if len(pieces) > 0:
        values = level_of(own_key, dims, pieces, -0.22, 0.18) * values
    return jnp.clip(values, min=-most, max=most).astype(dtype)


def setup_inputs(seed: int = 0) -> dict:
    keys = jax.random.split(jax.random.key(seed), 6)
    sources = noise(keys[0], (LAYERS, TOKENS, D), 1.0, 6.0, ((0, 4), (1, 64)))
    targets = noise(keys[1], (LAYERS, TOKENS, D), 1.0, 6.0, ((0, 4), (1, 64)))
    enc_weight = noise(keys[2], (LAYERS, F, D), D ** -0.5, 0.09375, ((0, 4), (1, 64)))
    dec_weight = noise(keys[3], (LAYERS, LAYERS, F, D), F ** -0.5, 0.0625, ((0, 4), (2, 64)))
    active = set_ends((jax.random.randint(keys[4], (LAYERS, F, TOKENS), 0, 5) < 2).astype(jnp.int32), jax.random.fold_in(keys[4], 1), 0, 1)
    return dict(sources=sources, targets=targets, enc_weight=enc_weight, dec_weight=dec_weight, active=active)


def reference(sources, targets, enc_weight, dec_weight, active):
    pre_acts = jnp.einsum('lfd,ltd->lft', enc_weight.astype(jnp.float32), sources.astype(jnp.float32))
    features = (active.astype(jnp.float32) * pre_acts).astype(jnp.bfloat16)
    scale = 1.0 / math.sqrt(TOKENS)
    error_list = []
    for target in range(LAYERS):
        recon = jnp.zeros((TOKENS, D), jnp.float32)
        for source in range(target + 1):
            recon = recon + jnp.dot(features[source].T, dec_weight[target, source], preferred_element_type=jnp.float32)
        error_list.append(recon - targets[target].astype(jnp.float32))
    errors = jnp.stack(error_list)
    scaled_error = (errors * scale).astype(jnp.bfloat16)
    dec_rows = []
    for target in range(LAYERS):
        blocks = []
        for source in range(LAYERS):
            if source <= target:
                blocks.append(jnp.dot(features[source], scaled_error[target], preferred_element_type=jnp.float32).astype(jnp.bfloat16))
            else:
                blocks.append(jnp.zeros((F, D), jnp.bfloat16))
        dec_rows.append(jnp.stack(blocks))
    grad_dec = jnp.stack(dec_rows)
    enc_list = []
    for source in range(LAYERS):
        feature_grad = jnp.zeros((F, TOKENS), jnp.float32)
        for target in range(source, LAYERS):
            feature_grad = feature_grad + jnp.dot(dec_weight[target, source], scaled_error[target].T, preferred_element_type=jnp.float32)
        pre_grad = (active[source].astype(jnp.float32) * feature_grad).astype(jnp.bfloat16)
        enc_list.append(jnp.dot(pre_grad, sources[source], preferred_element_type=jnp.float32).astype(jnp.bfloat16))
    grad_enc = jnp.stack(enc_list)
    return (errors, grad_dec, grad_enc)
```

```python
import math

import jax
import jax.numpy as jnp
from jax import lax
from jax.sharding import Mesh, PartitionSpec as P

TOKENS = 512
SIZES = {"xl": 2, "c": 2, "xh": 2, "z": 8, "y": 4}
LAYER = ("xl", "c")
FEAT = ("xh", "z", "y")
BF = jnp.bfloat16
F32 = jnp.float32


def fetch(x, axis, step):
    n = SIZES[axis]
    return lax.ppermute(x, axis, [(k, (k - step) % n) for k in range(n)])


def send(x, axis, step):
    return fetch(x, axis, -step)


def ring_gather(x):
    half = x.shape[-1] // 2
    up, down = [x], [x]
    for _ in range(3):
        up.append(fetch(up[-1], "z", 1))
        down.append(fetch(down[-1], "z", -1))
    far = jnp.concatenate(
        [fetch(up[3][..., :half], "z", 1), fetch(down[3][..., half:], "z", -1)], axis=-1
    )
    return jnp.stack([x, up[1], up[2], up[3], far, down[3], down[2], down[1]])


def direct_gather(x, axis, at):
    return jnp.stack([x] + [fetch(x, axis, j) for j in range(1, SIZES[axis])], axis=at)


def gather_a(x):
    x = direct_gather(x, "y", 0)
    x = direct_gather(x, "xh", 0)
    return ring_gather(x)


def gather_b(x):
    x = ring_gather(x)
    x = direct_gather(x, "xh", 1)
    return direct_gather(x, "y", 2)


def direct_reduce(parts, axis):
    total = parts[0].astype(F32)
    for j in range(1, SIZES[axis]):
        total = total + send(parts[j].astype(BF), axis, j).astype(F32)
    return total


def ring_reduce(parts):
    half = parts[0].shape[-1] // 2

    def add(a, b):
        return (a.astype(F32) + b.astype(F32)).astype(BF)

    up = send(parts[4][..., :half], "z", 1)
    down = send(parts[4][..., half:], "z", -1)
    up = jnp.concatenate([add(up, parts[3][..., :half]), parts[3][..., half:]], axis=-1)
    down = jnp.concatenate([parts[5][..., :half], add(down, parts[5][..., half:])], axis=-1)
    for j in (2, 1):
        up = add(send(up, "z", 1), parts[j])
        down = add(send(down, "z", -1), parts[8 - j])
    up = send(up, "z", 1)
    down = send(down, "z", -1)
    return parts[0].astype(F32) + up.astype(F32) + down.astype(F32)


def reduce_a(x):
    x = ring_reduce([x[j] for j in range(8)])
    x = direct_reduce([x[0], x[1]], "xh")
    return direct_reduce([x[j] for j in range(4)], "y")


def reduce_b(x):
    x = direct_reduce([x[:, :, j] for j in range(4)], "y")
    x = direct_reduce([x[:, 0], x[:, 1]], "xh")
    return direct_reduce([x[j] for j in range(8)], "z")


def on_device(sources, targets, enc_weight, dec_weight, active):
    sources, targets, enc_weight = sources[0], targets[0], enc_weight[0]
    dec_weight, active = dec_weight[0], active[0]
    block, width = sources.shape
    half = width // 2
    xl, core = lax.axis_index("xl"), lax.axis_index("c")
    layer = xl * 2 + core
    xh, z, y = lax.axis_index("xh"), lax.axis_index("z"), lax.axis_index("y")

    place = lax.broadcasted_iota(jnp.int32, (TOKENS, TOKENS), 1)
    row, dy = place % 8, (place // 8) % 4
    dxh, dz = (place // 32) % 2, place // 64
    token = (((xh + dxh) % 2) * 32 + ((z + dz) % 8) * 4 + (y + dy) % 4) * 8 + row
    order = (lax.broadcasted_iota(jnp.int32, (TOKENS, TOKENS), 0) == token).astype(BF)
    gate = jnp.dot(active.astype(BF), order, preferred_element_type=F32)

    src_a = gather_a(sources[:, :half]).reshape(TOKENS, half)
    src_b = gather_b(sources[:, half:]).reshape(TOKENS, half)
    contract = (((1,), (1,)), ((), ()))
    pre_acts = lax.dot_general(
        enc_weight[:, :half], src_a, contract, preferred_element_type=F32
    ) + lax.dot_general(enc_weight[:, half:], src_b, contract, preferred_element_type=F32)
    features = (gate * pre_acts).astype(BF)
    all_features = lax.all_gather(features, LAYER, axis=0)
    causal = jnp.arange(4, dtype=jnp.int32) <= layer
    masked = all_features * causal[:, None, None].astype(BF)

    def recon_of(dec):
        return (
            jnp.einsum("lft,lfd->td", masked, dec, preferred_element_type=F32)
            .astype(BF)
            .reshape(8, 2, 4, block, half)
        )

    recon = jnp.concatenate(
        [reduce_a(recon_of(dec_weight[:, :, :half])), reduce_b(recon_of(dec_weight[:, :, half:]))],
        axis=-1,
    )
    errors = recon - targets.astype(F32)
    scaled = (errors * (1.0 / math.sqrt(TOKENS))).astype(BF)
    err_a = gather_a(scaled[:, :half]).reshape(TOKENS, half)
    err_b = gather_b(scaled[:, half:]).reshape(TOKENS, half)

    grad_dec = jnp.concatenate(
        [
            jnp.einsum("lft,td->lfd", masked, err, preferred_element_type=F32).astype(BF)
            for err in (err_a, err_b)
        ],
        axis=-1,
    )
    partial = jnp.einsum(
        "lfd,td->lft", dec_weight[:, :, :half], err_a, preferred_element_type=F32
    ) + jnp.einsum("lfd,td->lft", dec_weight[:, :, half:], err_b, preferred_element_type=F32)
    partial = partial * causal[:, None, None].astype(F32)

    pairs = partial.reshape(2, 2, *partial.shape[1:])
    mine = jnp.where(core == 0, pairs[:, 0], pairs[:, 1])
    other = jnp.where(core == 0, pairs[:, 1], pairs[:, 0])
    mine = mine + send(other, "c", 1)
    keep = jnp.where(xl == 0, mine[0], mine[1])
    give = jnp.where(xl == 0, mine[1], mine[0])
    feature_grad = keep + send(give, "xl", 1)

    pre_grad = (gate * feature_grad).astype(BF)
    grad_enc = jnp.concatenate(
        [
            jnp.dot(pre_grad, src, preferred_element_type=F32).astype(BF)
            for src in (src_a, src_b)
        ],
        axis=-1,
    )
    return errors[None], grad_dec[None], grad_enc[None]


def solution(mesh):
    fine = Mesh(mesh.devices.reshape(tuple(SIZES.values())), tuple(SIZES))
    rows = P(LAYER, FEAT, None)
    panel = P(LAYER, None, FEAT, None)
    return jax.shard_map(
        on_device,
        mesh=fine,
        in_specs=(rows, rows, rows, panel, rows),
        out_specs=(rows, panel, rows),
        check_vma=False,
    )
```

```python
import math

import jax
import jax.numpy as jnp
from jax import lax
from jax.sharding import Mesh, PartitionSpec as P

TOKENS = 512
SIZES = {"xl": 2, "c": 2, "xh": 2, "z": 8, "y": 4}
LAYER = ("xl", "c")
FEAT = ("xh", "z", "y")
BF = jnp.bfloat16
F32 = jnp.float32


def fetch(x, axis, step):
    n = SIZES[axis]
    return lax.ppermute(x, axis, [(k, (k - step) % n) for k in range(n)])


def send(x, axis, step):
    return fetch(x, axis, -step)


def ring_gather(x, at):
    half = x.shape[-1] // 2
    up, down = [x], [x]
    for _ in range(3):
        up.append(fetch(up[-1], "z", 1))
        down.append(fetch(down[-1], "z", -1))
    far = jnp.concatenate(
        [fetch(up[3][..., :half], "z", 1), fetch(down[3][..., half:], "z", -1)], axis=-1
    )
    return jnp.stack([x, up[1], up[2], up[3], far, down[3], down[2], down[1]], axis=at)


def direct_gather(x, axis, at):
    return jnp.stack([x] + [fetch(x, axis, j) for j in range(1, SIZES[axis])], axis=at)


def doubling_gather(x):
    x = jnp.stack([x, fetch(x, "z", 4)])
    x = jnp.concatenate([x, fetch(x, "z", -2)])
    x = jnp.concatenate([x, fetch(x, "z", 1)])
    return jnp.stack([x[j] for j in (0, 4, 3, 7, 1, 5, 2, 6)])


def gather_a(x, whole=True):
    x = direct_gather(x, "y", 0)
    if whole:
        x = direct_gather(x, "xh", 1)
    return ring_gather(x, x.ndim - 2)


def gather_b(x, whole=True):
    x = doubling_gather(x)
    if whole:
        x = direct_gather(x, "xh", 0)
    return direct_gather(x, "y", 0)


def direct_reduce(parts, axis):
    total = parts[0].astype(F32)
    for j in range(1, SIZES[axis]):
        total = total + send(parts[j].astype(BF), axis, j).astype(F32)
    return total


def add(a, b):
    return (a.astype(F32) + b.astype(F32)).astype(BF)


def doubling_reduce(x):
    def step(kept, given, shift):
        return kept + send(given.astype(BF), "z", shift).astype(F32)

    x = step(
        jnp.stack([x[0], x[4], x[2], x[6]]), jnp.stack([x[1], x[5], x[3], x[7]]), 1
    )
    x = step(x[:2], jnp.stack([x[3], x[2]]), -2)
    return step(x[0], x[1], 4)


def reduce(a, b):
    half = a.shape[-1] // 2
    b_y = []
    for j in (1, 3, 2):
        b_y.append(send(b[j], "y", j))
    up = send(a[:, :, 4, :, :half], "z", 1)
    down = send(a[:, :, 4, :, half:], "z", -1)
    up, down = lax.optimization_barrier((up, down))
    up = jnp.concatenate([add(up, a[:, :, 3, :, :half]), a[:, :, 3, :, half:]], axis=-1)
    down = jnp.concatenate([a[:, :, 5, :, :half], add(down, a[:, :, 5, :, half:])], axis=-1)
    up, down = send(up, "z", 1), send(down, "z", -1)
    up, down = lax.optimization_barrier((up, down))
    up, down = send(add(up, a[:, :, 2]), "z", 1), send(add(down, a[:, :, 6]), "z", -1)
    up, down = lax.optimization_barrier((up, down))
    up, down = add(up, a[:, :, 1]), add(down, a[:, :, 7])
    up, down = send(up, "z", 1), send(down, "z", -1)
    b = b[0].astype(F32) + sum(part.astype(F32) for part in b_y)
    b_x = send(b[1].astype(BF), "xh", 1)
    a = a[:, :, 0].astype(F32) + up.astype(F32) + down.astype(F32)
    a = direct_reduce([a[:, 0], a[:, 1]], "xh")
    a = direct_reduce([a[j] for j in range(4)], "y")
    return jnp.concatenate([a, doubling_reduce(b[0] + b_x.astype(F32))], axis=-1)


def step(sources, targets, enc_weight, dec_weight, active):
    sources, targets, enc_weight = sources[0], targets[0], enc_weight[0]
    dec_weight, active = dec_weight[0], active[0]
    block, width = sources.shape
    half = width // 2
    xl, core = lax.axis_index("xl"), lax.axis_index("c")
    layer = xl * 2 + core
    xh, z, y = lax.axis_index("xh"), lax.axis_index("z"), lax.axis_index("y")

    place = lax.broadcasted_iota(jnp.int32, (TOKENS, TOKENS), 1)
    row, dz = place % 8, (place // 8) % 8
    dxh, dy = (place // 64) % 2, place // 128
    token = (((xh + dxh) % 2) * 32 + ((z + dz) % 8) * 4 + (y + dy) % 4) * 8 + row
    order = (lax.broadcasted_iota(jnp.int32, (TOKENS, TOKENS), 0) == token).astype(BF)
    gate = jnp.dot(active.astype(BF), order, preferred_element_type=F32)

    both = jnp.stack([enc_weight, fetch(enc_weight, "xh", 1)])
    src_a = gather_a(sources[:, :half], whole=False).reshape(TOKENS // 2, half)
    src_b = gather_b(sources[:, half:], whole=False).reshape(TOKENS // 2, half)
    pre_acts = jnp.einsum(
        "pfd,td->pft", both[:, :, :half], src_a, preferred_element_type=F32
    ) + jnp.einsum("pfd,td->pft", both[:, :, half:], src_b, preferred_element_type=F32)
    pre_acts = pre_acts.astype(BF)
    pre_acts = jnp.concatenate([pre_acts[0], fetch(pre_acts[1], "xh", 1)], axis=-1)
    came = lax.broadcasted_iota(jnp.int32, (TOKENS, TOKENS), 0)
    goes = ((came // 64) % 4) * 128 + (came // 256) * 64 + came % 64
    pre_acts = jnp.dot(pre_acts, (goes == place).astype(BF), preferred_element_type=F32)
    features = (gate * pre_acts).astype(BF)
    all_features = lax.all_gather(features, LAYER, axis=0)
    causal = jnp.arange(4, dtype=jnp.int32) <= layer
    masked = all_features * causal[:, None, None].astype(BF)

    def recon_of(used, dec):
        recon = jnp.einsum("lft,lfd->td", used, dec, preferred_element_type=F32)
        return recon.astype(BF)

    recon_a = recon_of(masked, dec_weight[:, :, :half]).reshape(4, 2, 8, block, half)
    recon_b = [
        recon_of(masked[:, :, 128 * k : 128 * (k + 1)], dec_weight[:, :, half:]).reshape(
            2, 8, block, half
        )
        for k in range(4)
    ]
    recon = reduce(recon_a, recon_b)
    rest_a = fetch(src_a, "xh", 1)
    rest_b = fetch(src_b, "xh", 1)
    src_a, src_b = (
        jnp.stack([own.reshape(4, 64, half), rest.reshape(4, 64, half)], axis=1).reshape(
            TOKENS, half
        )
        for own, rest in ((src_a, rest_a), (src_b, rest_b))
    )
    errors = recon - targets.astype(F32)
    scaled = (errors * (1.0 / math.sqrt(TOKENS))).astype(BF)
    err_a = gather_a(scaled[:, :half]).reshape(TOKENS, half)
    err_b = gather_b(scaled[:, half:]).reshape(TOKENS, half)

    grad_dec = jnp.concatenate(
        [
            jnp.einsum("lft,td->lfd", masked, err, preferred_element_type=F32).astype(BF)
            for err in (err_a, err_b)
        ],
        axis=-1,
    )
    partial = jnp.einsum(
        "lfd,td->lft", dec_weight[:, :, :half], err_a, preferred_element_type=F32
    ) + jnp.einsum("lfd,td->lft", dec_weight[:, :, half:], err_b, preferred_element_type=F32)
    partial = partial * causal[:, None, None].astype(F32)

    pairs = partial.reshape(2, 2, *partial.shape[1:])
    mine = jnp.where(core == 0, pairs[:, 0], pairs[:, 1])
    other = jnp.where(core == 0, pairs[:, 1], pairs[:, 0])
    mine = mine + send(other, "c", 1)
    keep = jnp.where(xl == 0, mine[0], mine[1])
    give = jnp.where(xl == 0, mine[1], mine[0])
    feature_grad = keep + send(give.astype(BF), "xl", 1).astype(F32)

    pre_grad = (gate * feature_grad).astype(BF)
    grad_enc = jnp.concatenate(
        [
            jnp.dot(pre_grad, src, preferred_element_type=F32).astype(BF)
            for src in (src_a, src_b)
        ],
        axis=-1,
    )
    return errors[None], grad_dec[None], grad_enc[None]


def solution(mesh):
    fine = Mesh(mesh.devices.reshape(tuple(SIZES.values())), tuple(SIZES))
    rows = P(LAYER, FEAT, None)
    panel = P(LAYER, None, FEAT, None)
    return jax.shard_map(
        step,
        mesh=fine,
        in_specs=(rows, rows, rows, panel, rows),
        out_specs=(rows, panel, rows),
        check_vma=False,
    )
```

```python
import math

import jax
import jax.numpy as jnp
from jax import lax
from jax.sharding import Mesh, PartitionSpec as P

TOKENS = 512
SIZES = {"xl": 2, "c": 2, "xh": 2, "z": 8, "y": 4}
LAYER = ("xl", "c")
FEAT = ("xh", "z", "y")
BF = jnp.bfloat16
F32 = jnp.float32


def fetch(x, axis, step):
    n = SIZES[axis]
    return lax.ppermute(x, axis, [(k, (k - step) % n) for k in range(n)])


def send(x, axis, step):
    return fetch(x, axis, -step)


def ring_gather(x, at):
    half = x.shape[-1] // 2
    up, down = [x], [x]
    for _ in range(3):
        up.append(fetch(up[-1], "z", 1))
        down.append(fetch(down[-1], "z", -1))
    far = jnp.concatenate(
        [fetch(up[3][..., :half], "z", 1), fetch(down[3][..., half:], "z", -1)], axis=-1
    )
    return jnp.stack([x, up[1], up[2], up[3], far, down[3], down[2], down[1]], axis=at)


def direct_gather(x, axis, at):
    return jnp.stack([x] + [fetch(x, axis, j) for j in range(1, SIZES[axis])], axis=at)


def doubling_gather(x):
    far = fetch(x, "z", 4)
    x = jnp.stack([x, far])
    x = jnp.concatenate([x, fetch(x, "z", -2)])
    near = fetch(x, "z", 1)
    x = jnp.concatenate([x, near])
    return jnp.stack([x[j] for j in (0, 4, 3, 7, 1, 5, 2, 6)])


def gather_a(x, whole=True):
    parts = [fetch(x, "y", j) for j in (1, 2, 3)]
    x = jnp.stack([x, *parts])
    if whole:
        part = fetch(x, "xh", 1)
        x = jnp.stack([x, part], axis=1)
    return ring_gather(x, x.ndim - 2)


def gather_b(x, whole=True):
    x = doubling_gather(x)
    if whole:
        x = direct_gather(x, "xh", 0)
    return direct_gather(x, "y", 0)


def direct_reduce(parts, axis):
    total = parts[0].astype(F32)
    for j in range(1, SIZES[axis]):
        total = total + send(parts[j].astype(BF), axis, j).astype(F32)
    return total


def add(a, b):
    return (a.astype(F32) + b.astype(F32)).astype(BF)


def doubling_reduce(x):
    def step(kept, given, shift):
        return kept + send(given.astype(BF), "z", shift).astype(F32)

    x = step(
        jnp.stack([x[0], x[4], x[2], x[6]]), jnp.stack([x[1], x[5], x[3], x[7]]), 1
    )
    x = step(x[:2], jnp.stack([x[3], x[2]]), -2)
    return step(x[0], x[1], 4)


def reduce(a, b):
    half = a.shape[-1] // 2
    b_y = []
    for j in (1, 2, 3):
        b_y.append(send(b[j], "y", j))
    up = send(a[:, :, 4, :, :half], "z", 1)
    down = send(a[:, :, 4, :, half:], "z", -1)
    up, down = lax.optimization_barrier((up, down))
    up = jnp.concatenate([add(up, a[:, :, 3, :, :half]), a[:, :, 3, :, half:]], axis=-1)
    down = jnp.concatenate([a[:, :, 5, :, :half], add(down, a[:, :, 5, :, half:])], axis=-1)
    up, down = send(up, "z", 1), send(down, "z", -1)
    up, down = lax.optimization_barrier((up, down))
    up, down = add(up, a[:, :, 2]), add(down, a[:, :, 6])
    up, down = send(up, "z", 1), send(down, "z", -1)
    up, down = lax.optimization_barrier((up, down))
    up, down = add(up, a[:, :, 1]), add(down, a[:, :, 7])
    up, down = send(up, "z", 1), send(down, "z", -1)
    b = b[0].astype(F32) + sum(part.astype(F32) for part in b_y)
    b_x = send(b[1].astype(BF), "xh", 1)
    a = a[:, :, 0].astype(F32) + up.astype(F32) + down.astype(F32)
    a = direct_reduce([a[:, 0], a[:, 1]], "xh")
    a = direct_reduce([a[j] for j in range(4)], "y")
    return jnp.concatenate([a, doubling_reduce(b[0] + b_x.astype(F32))], axis=-1)


def step(sources, targets, enc_weight, dec_weight, active):
    sources, targets, enc_weight = sources[0], targets[0], enc_weight[0]
    dec_weight, active = dec_weight[0], active[0]
    block, width = sources.shape
    half = width // 2
    xl, core = lax.axis_index("xl"), lax.axis_index("c")
    layer = xl * 2 + core
    xh, z, y = lax.axis_index("xh"), lax.axis_index("z"), lax.axis_index("y")

    place = lax.broadcasted_iota(jnp.int32, (TOKENS, TOKENS), 1)
    row, dz = place % 8, (place // 8) % 8
    dxh, dy = (place // 64) % 2, place // 128
    token = (((xh + dxh) % 2) * 32 + ((z + dz) % 8) * 4 + (y + dy) % 4) * 8 + row
    order = (lax.broadcasted_iota(jnp.int32, (TOKENS, TOKENS), 0) == token).astype(BF)
    gate = jnp.dot(active.astype(BF), order, preferred_element_type=F32)

    both = jnp.stack([enc_weight, fetch(enc_weight, "xh", 1)])
    src_a = gather_a(sources[:, :half], whole=False).reshape(TOKENS // 2, half)
    src_b = gather_b(sources[:, half:], whole=False).reshape(TOKENS // 2, half)
    pre_acts = jnp.einsum(
        "pfd,td->pft", both[:, :, :half], src_a, preferred_element_type=F32
    ) + jnp.einsum("pfd,td->pft", both[:, :, half:], src_b, preferred_element_type=F32)
    pre_acts = pre_acts.astype(BF)
    pre_acts = jnp.concatenate([pre_acts[0], fetch(pre_acts[1], "xh", 1)], axis=-1)
    came = lax.broadcasted_iota(jnp.int32, (TOKENS, TOKENS), 0)
    goes = ((came // 64) % 4) * 128 + (came // 256) * 64 + came % 64
    pre_acts = jnp.dot(pre_acts, (goes == place).astype(BF), preferred_element_type=F32)
    features = (gate * pre_acts).astype(BF)
    all_features = lax.all_gather(features, LAYER, axis=0)
    causal = jnp.arange(4, dtype=jnp.int32) <= layer
    masked = all_features * causal[:, None, None].astype(BF)

    def recon_of(used, dec):
        recon = jnp.einsum("lft,lfd->td", used, dec, preferred_element_type=F32)
        return recon.astype(BF)

    recon_a = recon_of(masked, dec_weight[:, :, :half]).reshape(4, 2, 8, block, half)
    recon_b = [
        recon_of(masked[:, :, 128 * k : 128 * (k + 1)], dec_weight[:, :, half:]).reshape(
            2, 8, block, half
        )
        for k in range(4)
    ]
    recon = reduce(recon_a, recon_b)
    rest_a = fetch(src_a, "xh", 1)
    rest_b = fetch(src_b, "xh", 1)
    src_a, src_b = (
        jnp.stack([own.reshape(4, 64, half), rest.reshape(4, 64, half)], axis=1).reshape(
            TOKENS, half
        )
        for own, rest in ((src_a, rest_a), (src_b, rest_b))
    )
    errors = recon - targets.astype(F32)
    scaled = (errors * (1.0 / math.sqrt(TOKENS))).astype(BF)
    err_a = gather_a(scaled[:, :half]).reshape(TOKENS, half)
    err_b = gather_b(scaled[:, half:]).reshape(TOKENS, half)

    grad_dec = jnp.concatenate(
        [
            jnp.einsum("lft,td->lfd", masked, err, preferred_element_type=F32).astype(BF)
            for err in (err_a, err_b)
        ],
        axis=-1,
    )
    partial = jnp.einsum(
        "lfd,td->lft", dec_weight[:, :, :half], err_a, preferred_element_type=F32
    ) + jnp.einsum("lfd,td->lft", dec_weight[:, :, half:], err_b, preferred_element_type=F32)
    partial = partial * causal[:, None, None].astype(F32)

    pairs = partial.reshape(2, 2, *partial.shape[1:])
    mine = jnp.where(core == 0, pairs[:, 0], pairs[:, 1])
    other = jnp.where(core == 0, pairs[:, 1], pairs[:, 0])
    came_in = send(other, "c", 1)
    mine = mine + came_in
    keep = jnp.where(xl == 0, mine[0], mine[1])
    give = jnp.where(xl == 0, mine[1], mine[0])
    feature_grad = keep + send(give.astype(BF), "xl", 1).astype(F32)

    pre_grad = (gate * feature_grad).astype(BF)
    grad_enc = jnp.concatenate(
        [
            jnp.dot(pre_grad, src, preferred_element_type=F32).astype(BF)
            for src in (src_a, src_b)
        ],
        axis=-1,
    )
    return errors[None], grad_dec[None], grad_enc[None]


def solution(mesh):
    fine = Mesh(mesh.devices.reshape(tuple(SIZES.values())), tuple(SIZES))
    rows = P(LAYER, FEAT, None)
    panel = P(LAYER, None, FEAT, None)
    return jax.shard_map(
        step,
        mesh=fine,
        in_specs=(rows, rows, rows, panel, rows),
        out_specs=(rows, panel, rows),
        check_vma=False,
    )
```
